32 devices in a mesh: row: 16 (over z, x, core), col: 2 (over y).
Axes of the slice: x: 2, y: 2, z: 4, core: 2. Of those that a mesh axis runs over, the one named last changes fastest.
Arguments:
- solution: float32 [8, 1024, 2048], P(None, 'row', 'col'), may hold values from -1 to 1, as said below
- search: float32 [8, 1024, 2048], P(None, 'row', 'col'), may hold values from -1 to 1, as said below
- basis: float32 [8, 1024, 2048], P(None, 'row', 'col'), may hold values from -1 to 1, as said below
- resid_a: float32 [1024, 2048], P('row', 'col'), may hold values from -1 to 1, as said below
- resid_b: float32 [1024, 2048], P('row', 'col'), may hold values from -1 to 1, as said below
- scalars: float32 [3], replicated, may hold values from 0.5 to 2
- profile_a: float32 [8, 512], replicated, may hold values from -0.25 to 0.25
- profile_b: float32 [8, 512], replicated, may hold values from -0.25 to 0.25
- source_mask: int32 [1024, 2048], P('row', 'col'), may hold values 0 or 1
- weight_code: int32 [1024, 2048], P('row', 'col'), may hold values from 0 to 7
- roll_code: int32 [1024, 2048], P('row', 'col'), may hold values from 0 to 2
Outputs:
- next_solution: float32 [8, 1024, 2048], P(None, 'row', 'col')
- next_search: float32 [8, 1024, 2048], P(None, 'row', 'col')
- next_basis: float32 [8, 1024, 2048], P(None, 'row', 'col')
- next_resid_a: float32 [1024, 2048], P('row', 'col')
- next_resid_b: float32 [1024, 2048], P('row', 'col')
The draws below stay inside these ranges and needn't reach their ends.
Inputs may be any that keep to these rules, and one draw needn't show every extreme that they name: `solution`: the whole array has Euclidean norm 1. `search`: the whole array has Euclidean norm 1. `basis`: the whole array has Euclidean norm 1. Euclidean norm sqrt(1/2), so that resid_a and resid_b together have norm 1. Euclidean norm sqrt(1/2), so that resid_a and resid_b together have norm 1.
All inputs are finite; a program needn't handle non-finite values. No bound on the sum of `source_mask` on one device may be relied on, other than what follows from the above.
Results may differ from the reference program's by a relative error of at most 0.000078.
Values sent between devices are 32-bit elements; how exact they have to be, the bound alone decides.
No kernel may reach another device: no remote copies, remote signals or barrier semaphores. Data moves between devices by JAX's collectives and lax.ppermute only.
A program may use at most 128 MiB of HBM per device.

```python
import jax
import jax.numpy as jnp
from jax import lax

K = 8
L = 512
NC = 2048
NR = 1024


def normed_field(key, shape, norm_value):
    values = jax.random.normal(key, shape, jnp.float32)
    return values * (norm_value / jnp.sqrt(jnp.sum(values * values)))


def draw_solution(key, part):
    return normed_field(jax.random.fold_in(key, 11), (K, NR, NC), 1.0)


def draw_search(key, part):
    return normed_field(jax.random.fold_in(key, 23), (K, NR, NC), 1.0)


def draw_basis(key, part):
    return normed_field(jax.random.fold_in(key, 37), (K, NR, NC), 1.0)


def draw_resid_a(key, part):
    return normed_field(jax.random.fold_in(key, 41), (NR, NC), 0.5 ** 0.5)


def draw_resid_b(key, part):
    return normed_field(jax.random.fold_in(key, 53), (NR, NC), 0.5 ** 0.5)


def plant(entries, stream_key, smallest, largest):
    extent = entries.shape
    place = [jax.random.randint(jax.random.fold_in(stream_key, axis), (), 0, extent[axis]) for axis in range(len(extent))]
    entries = entries.at[tuple(place)].set(smallest)
    longest = extent.index(max(extent))
    place[longest] = (place[longest] + 1) % extent[longest]
    return entries.at[tuple(place)].set(largest)


def gaussian(own_key, extent, spread, limit, dtype=jnp.bfloat16):
    entries = jax.random.normal(own_key, extent, jnp.float32) * spread
    return jnp.minimum(jnp.maximum(entries, -limit), limit).astype(dtype)


def setup_inputs(seed: int = 0) -> dict:
    splits = jax.random.split(jax.random.key(seed), 12)
    solution = draw_solution(jax.random.fold_in(splits[11], 71), 0)
    search = draw_search(jax.random.fold_in(splits[11], 71), 0)
    basis = draw_basis(jax.random.fold_in(splits[11], 71), 0)
    resid_a = draw_resid_a(jax.random.fold_in(splits[11], 71), 0)
    resid_b = draw_resid_b(jax.random.fold_in(splits[11], 71), 0)
    scalars = jnp.clip(jax.random.uniform(splits[5], (3,), jnp.float32, 0.5, 2.0), 0.5, 2.0)
    profile_a = gaussian(splits[6], (K, L), L ** -0.5, 0.25, jnp.float32)
    profile_b = gaussian(splits[7], (K, L), L ** -0.5, 0.25, jnp.float32)
    source_mask = plant((jax.random.randint(splits[8], (NR, NC), 0, 4) < 3).astype(jnp.int32), jax.random.fold_in(splits[8], 1), 0, 1)
    weight_code = plant(jax.random.randint(splits[9], (NR, NC), 0, 8), jax.random.fold_in(splits[9], 1), 0, 7).astype(jnp.int32)
    roll_code = plant(jax.random.randint(splits[10], (NR, NC), 0, 3), jax.random.fold_in(splits[10], 1), 0, 2).astype(jnp.int32)
    return {"solution": solution, "search": search, "basis": basis, "resid_a": resid_a, "resid_b": resid_b, "scalars": scalars, "profile_a": profile_a, "profile_b": profile_b, "source_mask": source_mask, "weight_code": weight_code, "roll_code": roll_code}


epsilon = 1e-12

def roll_weights(weight_code, roll_code):
    base = 1.0 / (1.0 + 0.25 * weight_code.astype(jnp.float32))
    return (base * (roll_code != 2).astype(jnp.float32), base * (roll_code != 1).astype(jnp.float32))

def forward(maps, masked, weight_a, weight_b, profile_a, profile_b):
    source = maps * masked[None]
    length = profile_a.shape[1]
    rows_all = source.shape[1]
    cols_all = source.shape[2]
    total = cols_all + length
    spectrum = jnp.fft.rfft(source, n=total, axis=2)
    kernel = jnp.fft.rfft(profile_a, n=total, axis=1)
    image_a = jnp.fft.irfft(lax.optimization_barrier(jnp.sum(spectrum * kernel[:, None, :], axis=0)), n=total, axis=1)[:, :cols_all]
    total = rows_all + length
    spectrum = jnp.fft.rfft(source, n=total, axis=1)
    kernel = jnp.fft.rfft(profile_b, n=total, axis=1)
    image_b = jnp.fft.irfft(lax.optimization_barrier(jnp.sum(spectrum * kernel[:, :, None], axis=0)), n=total, axis=0)[:rows_all]
    return (weight_a * image_a, weight_b * image_b)

def adjoint(first, second, masked, weight_a, weight_b, profile_a, profile_b):
    length = profile_a.shape[1]
    rows_all, cols_all = first.shape
    total = cols_all + length
    spectrum = jnp.fft.rfft(weight_a * first, n=total, axis=1)
    kernel = jnp.conj(jnp.fft.rfft(profile_a, n=total, axis=1))
    grad_a = jnp.fft.irfft(spectrum[None] * kernel[:, None, :], n=total, axis=2)[:, :, :cols_all]
    total = rows_all + length
    spectrum = jnp.fft.rfft(weight_b * second, n=total, axis=0)
    kernel = jnp.conj(jnp.fft.rfft(profile_b, n=total, axis=1))
    grad_b = jnp.fft.irfft(spectrum[None] * kernel[:, :, None], n=total, axis=1)[:, :rows_all]
    return masked[None] * (grad_a + grad_b)

def reference(solution, search, basis, resid_a, resid_b, scalars, profile_a, profile_b, source_mask, weight_code, roll_code):
    alpha = scalars[0]
    phibar = scalars[1]
    rhobar = scalars[2]
    weight_a, weight_b = roll_weights(weight_code, roll_code)
    masked = source_mask.astype(jnp.float32)
    image_a, image_b = forward(basis, masked, weight_a, weight_b, profile_a, profile_b)
    raw_a = image_a - alpha * resid_a
    raw_b = image_b - alpha * resid_b
    beta = jnp.sqrt(jnp.sum(raw_a * raw_a) + jnp.sum(raw_b * raw_b) + epsilon)
    next_resid_a = raw_a / beta
    next_resid_b = raw_b / beta
    raw_v = adjoint(next_resid_a, next_resid_b, masked, weight_a, weight_b, profile_a, profile_b) - beta * basis
    alpha_next = jnp.sqrt(jnp.sum(raw_v * raw_v) + epsilon)
    next_basis = raw_v / alpha_next
    rho_total = jnp.sqrt(rhobar * rhobar + beta * beta)
    cosine = rhobar / rho_total
    sine = beta / rho_total
    theta = sine * alpha_next
    phi_value = cosine * phibar
    next_solution = solution + phi_value / rho_total * search
    next_search = next_basis - theta / rho_total * search
    return (next_solution, next_search, next_basis, next_resid_a, next_resid_b)
```

```python
import functools
import math

import jax
import jax.numpy as jnp
from jax import lax
from jax.experimental import pallas as pl
from jax.experimental.pallas import tpu as pltpu
from jax.sharding import PartitionSpec as P

epsilon = 1e-12
LANES = 128
VMEM_BYTES = 40 * 1024 * 1024


def split(values):
    high = values.astype(jnp.bfloat16)
    return high, (values - high.astype(jnp.float32)).astype(jnp.bfloat16)


def dot3(left, right, dims):
    def dot(a, b):
        return lax.dot_general(a, b, (dims, ((), ())), preferred_element_type=jnp.float32)

    return dot(left[0], right[0]) + (dot(left[0], right[1]) + dot(left[1], right[0]))


def band_tiles(profile_ref, k, rows):
    length = profile_ref.shape[1]
    count = length // LANES
    row = lax.broadcasted_iota(jnp.int32, (rows, LANES), 0)
    lane = lax.broadcasted_iota(jnp.int32, (rows, LANES), 1)
    zero = jnp.zeros((rows, LANES), jnp.float32)
    rolled = []
    for e in range(count):
        piece = profile_ref[k : k + 1, e * LANES : (e + 1) * LANES]
        wide = jnp.broadcast_to(piece, (rows, LANES))
        rolled.append(pltpu.roll(wide, 0, 1, stride=1, stride_axis=0))
    inside = lane >= row
    for e in range(count + 1):
        ahead = rolled[e] if e < count else zero
        behind = rolled[e - 1] if e > 0 else zero
        yield e, jnp.where(inside, ahead, behind)


def rows_forward_kernel(depth, place_ref, basis_ref, mask_ref, profile_ref, keep_ref, send_ref, high_ref, low_ref):
    maps, rows, width = basis_ref.shape

    @pl.when(pl.program_id(0) == 0)
    def _():
        group = max(1, LANES // rows)
        for first in range(0, maps, group):
            members = [list(band_tiles(profile_ref, k, rows)) for k in range(first, first + group)]
            for e in range(len(members[0])):
                tile = jnp.concatenate([member[e][1] for member in members], axis=0)
                high, low = split(tile.T)
                place = (slice(e * LANES, (e + 1) * LANES), slice(first * rows, (first + group) * rows))
                high_ref[place] = high
                low_ref[place] = low

    masked = mask_ref[...].astype(jnp.float32)
    source = (basis_ref[...] * masked[None]).reshape(maps * rows, width)
    used = (depth + 1) * rows
    table = (high_ref[:used], low_ref[:used])
    total = dot3(table, split(source), ((1,), (0,)))
    core = place_ref[0]
    pairs = send_ref.shape[0]
    send_ref[pl.ds((pairs - 1) * (1 - core), 1)] = jnp.zeros((1, rows, width), jnp.float32)
    for d in range(depth + 1):
        block = total[d * rows : (d + 1) * rows]
        if d % 2 == 0:
            keep_ref[d // 2] = block
        else:
            send_ref[pl.ds(d // 2 + core, 1)] = block[None]


def rows_forward(basis, mask, profile, place, depth):
    maps, rows, columns = basis.shape
    width = math.gcd(256, columns)
    table_rows = (profile.shape[1] // LANES + 1) * LANES
    pairs = (depth + 1) // 2 + 1
    block = pl.BlockSpec((pairs, rows, width), lambda i, place: (0, 0, i))
    return pl.pallas_call(
        functools.partial(rows_forward_kernel, depth),
        grid_spec=pltpu.PrefetchScalarGridSpec(
            num_scalar_prefetch=1,
            grid=(columns // width,),
            in_specs=[
                pl.BlockSpec((maps, rows, width), lambda i, place: (0, 0, i)),
                pl.BlockSpec((rows, width), lambda i, place: (0, i)),
                pl.BlockSpec(profile.shape, lambda i, place: (0, 0)),
            ],
            out_specs=[block, block],
            scratch_shapes=[pltpu.VMEM((table_rows, maps * rows), jnp.bfloat16)] * 2,
        ),
        out_shape=[jax.ShapeDtypeStruct((pairs, rows, columns), jnp.float32)] * 2,
        compiler_params=pltpu.CompilerParams(vmem_limit_bytes=VMEM_BYTES),
        cost_estimate=pl.CostEstimate(
            flops=6 * (depth + 1) * rows * maps * rows * columns,
            bytes_accessed=4 * (maps + 1 + 2 * pairs) * rows * columns,
            transcendentals=0,
        ),
        name="rows_forward",
    )(place, basis, mask, profile)


def cols_forward_kernel(basis_ref, mask_ref, profile_ref, own_ref, halo_ref, high_ref, low_ref, left_high, left_low, total):
    maps, rows, columns = basis_ref.shape
    for k in range(maps):
        for e, tile in band_tiles(profile_ref, k, LANES):
            high, low = split(tile)
            place = (slice(k * LANES, (k + 1) * LANES), slice(e * LANES, (e + 1) * LANES))
            high_ref[place] = high
            low_ref[place] = low
    blocks = columns // LANES
    for n in range(blocks):
        lanes = slice(n * LANES, (n + 1) * LANES)
        masked = mask_ref[:, lanes].astype(jnp.float32)
        for k in range(maps):
            high, low = split(basis_ref[k, :, lanes] * masked)
            place = (slice(n * rows, (n + 1) * rows), slice(k * LANES, (k + 1) * LANES))
            left_high[place] = high
            left_low[place] = low
    reach = high_ref.shape[1]
    total[...] = jnp.zeros_like(total)
    spread = dot3((left_high[...], left_low[...]), (high_ref[...], low_ref[...]), ((1,), (0,)))
    for n in range(blocks):
        total[:, n * LANES : n * LANES + reach] += spread[n * rows : (n + 1) * rows]
    own_ref[...] = total[:, :columns]
    halo_ref[...] = total[:, columns:]


def cols_forward(basis, mask, profile):
    maps, rows, columns = basis.shape
    length = profile.shape[1]
    reach = length + LANES
    table = jax.ShapeDtypeStruct((maps * LANES, reach), jnp.bfloat16)
    stack = pltpu.VMEM((columns // LANES * rows, maps * LANES), jnp.bfloat16)
    return pl.pallas_call(
        cols_forward_kernel,
        out_shape=[
            jax.ShapeDtypeStruct((rows, columns), jnp.float32),
            jax.ShapeDtypeStruct((rows, length), jnp.float32),
            table,
            table,
        ],
        scratch_shapes=[stack, stack, pltpu.VMEM((rows, columns + length), jnp.float32)],
        compiler_params=pltpu.CompilerParams(vmem_limit_bytes=VMEM_BYTES),
        cost_estimate=pl.CostEstimate(
            flops=6 * rows * columns * maps * reach,
            bytes_accessed=4 * (maps + 3) * rows * columns,
            transcendentals=0,
        ),
        name="cols_forward",
    )(basis, mask, profile)


def cols_adjoint_kernel(image_ref, halo_ref, high_ref, low_ref, grad_ref, left_high, left_low):
    maps, rows, columns = grad_ref.shape
    reach = high_ref.shape[1]
    blocks = columns // LANES
    pieces = reach // LANES
    for b in range(blocks + pieces - 1):
        if b < blocks:
            tile = image_ref[:, b * LANES : (b + 1) * LANES]
        else:
            tile = halo_ref[:, (b - blocks) * LANES : (b - blocks + 1) * LANES]
        high, low = split(tile)
        for m in range(max(0, b - pieces + 1), min(blocks, b + 1)):
            place = (slice(m * rows, (m + 1) * rows), slice((b - m) * LANES, (b - m + 1) * LANES))
            left_high[place] = high
            left_low[place] = low
    for k in range(maps):
        band = slice(k * LANES, (k + 1) * LANES)
        spread = dot3((left_high[...], left_low[...]), (high_ref[band], low_ref[band]), ((1,), (1,)))
        for m in range(blocks):
            grad_ref[k, :, m * LANES : (m + 1) * LANES] = spread[m * rows : (m + 1) * rows]


def cols_adjoint(image, halo, high, low, maps):
    rows, columns = image.shape
    reach = high.shape[1]
    stack = pltpu.VMEM((columns // LANES * rows, reach), jnp.bfloat16)
    return pl.pallas_call(
        cols_adjoint_kernel,
        out_shape=jax.ShapeDtypeStruct((maps, rows, columns), jnp.float32),
        scratch_shapes=[stack, stack],
        compiler_params=pltpu.CompilerParams(vmem_limit_bytes=VMEM_BYTES),
        cost_estimate=pl.CostEstimate(
            flops=6 * rows * columns * maps * reach,
            bytes_accessed=4 * (maps + 3) * rows * columns,
            transcendentals=0,
        ),
        name="cols_adjoint",
    )(image, halo, high, low)


def rows_adjoint_kernel(evens, scale_ref, profile_ref, *refs):
    even_refs = refs[:evens]
    odd_ref, grad_ref, mask_ref, basis_ref, raw_ref, norm_ref, high_ref, low_ref, right_high, right_low = refs[evens:]
    maps, rows, width = grad_ref.shape
    depth = evens - 1 + odd_ref.shape[0]

    @pl.when(pl.program_id(0) == 0)
    def _():
        norm_ref[0, 0] = 0.0
        for k in range(maps):
            for e, tile in band_tiles(profile_ref, k, rows):
                high, low = split(tile)
                place = (slice(k * rows, (k + 1) * rows), slice(e * LANES, (e + 1) * LANES))
                high_ref[place] = high
                low_ref[place] = low
        filled = (depth + 1) * rows
        if right_high.shape[0] > filled:
            right_high[filled:] = jnp.zeros((right_high.shape[0] - filled, width), jnp.bfloat16)
            right_low[filled:] = jnp.zeros((right_high.shape[0] - filled, width), jnp.bfloat16)

    for d in range(depth + 1):
        high, low = split(even_refs[d // 2][...] if d % 2 == 0 else odd_ref[d // 2])
        right_high[d * rows : (d + 1) * rows] = high
        right_low[d * rows : (d + 1) * rows] = low
    table = (high_ref[...], low_ref[...])
    spread = dot3(table, (right_high[...], right_low[...]), ((1,), (0,)))
    beta = scale_ref[0]
    inverse = scale_ref[1]
    masked = mask_ref[...].astype(jnp.float32) * inverse
    raw = (spread.reshape(maps, rows, width) + grad_ref[...]) * masked[None] - beta * basis_ref[...]
    raw_ref[...] = raw
    norm_ref[0, 0] += jnp.sum(raw * raw)


def rows_adjoint(scale, profile, even, odd, grad, mask, basis):
    maps, rows, columns = basis.shape
    width = math.gcd(256, columns)
    reach = profile.shape[1] + LANES
    image = pl.BlockSpec((rows, width), lambda i, scale: (0, i))
    whole = pl.BlockSpec((maps, rows, width), lambda i, scale: (0, 0, i))
    return pl.pallas_call(
        functools.partial(rows_adjoint_kernel, len(even)),
        grid_spec=pltpu.PrefetchScalarGridSpec(
            num_scalar_prefetch=1,
            grid=(columns // width,),
            in_specs=[pl.BlockSpec(profile.shape, lambda i, scale: (0, 0))]
            + [image] * len(even)
            + [pl.BlockSpec((odd.shape[0], rows, width), lambda i, scale: (0, 0, i)), whole, image, whole],
            out_specs=[whole, pl.BlockSpec((1, 1), lambda i, scale: (0, 0), memory_space=pltpu.SMEM)],
            scratch_shapes=[pltpu.VMEM((maps * rows, reach), jnp.bfloat16)] * 2
            + [pltpu.VMEM((reach, width), jnp.bfloat16)] * 2,
        ),
        out_shape=[
            jax.ShapeDtypeStruct((maps, rows, columns), jnp.float32),
            jax.ShapeDtypeStruct((1, 1), jnp.float32),
        ],
        compiler_params=pltpu.CompilerParams(vmem_limit_bytes=VMEM_BYTES),
        cost_estimate=pl.CostEstimate(
            flops=6 * rows * columns * maps * reach,
            bytes_accessed=4 * (3 * maps + 12) * rows * columns,
            transcendentals=0,
        ),
        name="rows_adjoint",
    )(scale, profile, *even, odd, grad, mask, basis)


def shifted(block, axis, distance):
    devices = range(lax.axis_size(axis))
    return lax.ppermute(block, axis, [(i - distance, i) for i in devices if i - distance in devices])


def exchanged(block, axis, bit):
    return lax.ppermute(block, axis, [(i, i ^ bit) for i in range(lax.axis_size(axis))])


def total_over(value, axes):
    held = jnp.full((1, LANES), value, jnp.float32)
    for axis in axes:
        size = lax.axis_size(axis)
        bit = 1
        while bit < size:
            held = held + exchanged(held, axis, bit)
            bit *= 2
    return held[0, 0]


def total_at_once(value, axes):
    count = math.prod(lax.axis_size(axis) for axis in axes)
    copies = jnp.full((count, LANES), value, jnp.float32)
    return jnp.sum(lax.all_to_all(copies, axes, 0, 0, tiled=True)[:, 0])


def body(
    solution,
    search,
    basis,
    resid_a,
    resid_b,
    scalars,
    profile_a,
    profile_b,
    source_mask,
    weight_code,
    roll_code,
):
    alpha = scalars[0]
    phibar = scalars[1]
    rhobar = scalars[2]
    length = profile_a.shape[1]
    maps, rows_here, cols_here = basis.shape
    row_depth = -(-(length - 1) // rows_here)
    col_depth = -(-(length - 1) // cols_here)
    place = lax.axis_index("row")
    core = place % 2
    lower = (place // 2) % 2 == 0
    base = 1.0 / (1.0 + 0.25 * weight_code.astype(jnp.float32))
    weight_a = base * (roll_code != 2).astype(jnp.float32)
    weight_b = base * (roll_code != 1).astype(jnp.float32)

    keep, send = rows_forward(basis, source_mask, profile_b, core.reshape(1), row_depth)
    got = exchanged(send, "row", 1)
    pairs = [keep[m] + got[m] for m in range(keep.shape[0])]
    pair_depth = len(pairs) - 1
    four_depth = (pair_depth + 1) // 2
    zero = jnp.zeros((rows_here, cols_here), jnp.float32)
    odd_in = [zero] * (four_depth + 2)
    for m in reversed(range(1, pair_depth + 1, 2)):
        odd_in[m // 2 + 1] = exchanged(pairs[m], "row", 2)
    carried = zero
    for n in reversed(range(four_depth + 1)):
        mine = pairs[2 * n] if 2 * n <= pair_depth else zero
        level = mine + jnp.where(lower, odd_in[n], odd_in[n + 1])
        if n < four_depth:
            level = level + carried
        if n > 0:
            carried = shifted(level, "row", 4)
    image_b = level

    own, halo, table_high, table_low = cols_forward(basis, source_mask, profile_a)
    image_a = own
    for n in range(1, col_depth + 1):
        piece = halo[:, (n - 1) * cols_here : n * cols_here]
        piece = shifted(piece, "col", n)
        image_a = image_a + jnp.pad(piece, ((0, 0), (0, cols_here - piece.shape[1])))

    raw_a = weight_a * image_a - alpha * resid_a
    raw_b = weight_b * image_b - alpha * resid_b
    weighted_a = weight_a * raw_a
    weighted_b = weight_b * raw_b

    pieces = []
    for n in range(1, col_depth + 1):
        width = min(cols_here, length - (n - 1) * cols_here)
        pieces.append(shifted(weighted_a[:, :width], "col", -n))
    grad_a = cols_adjoint(weighted_a, jnp.concatenate(pieces, axis=1), table_high, table_low, maps)

    fours = [weighted_b]
    for n in range(four_depth):
        fours.append(shifted(fours[-1], "row", -4))
    evens = []
    for m in range(pair_depth + 1):
        if m % 2 == 0:
            evens.append(fours[m // 2])
        else:
            evens.append(exchanged(jnp.where(lower, fours[m // 2 + 1], fours[m // 2]), "row", 2))
    first = core == 0
    odd = jnp.stack([jnp.where(first, evens[m + 1], evens[m]) for m in range(pair_depth)])
    odd = exchanged(odd, "row", 1)

    square = total_over(jnp.sum(raw_a * raw_a) + jnp.sum(raw_b * raw_b), ("row", "col"))
    beta = jnp.sqrt(square + epsilon)
    scale = jnp.stack([beta, 1.0 / beta])
    raw_v, norm = rows_adjoint(scale, profile_b, evens, odd, grad_a, source_mask, basis)
    alpha_next = jnp.sqrt(total_at_once(norm[0, 0], ("row", "col")) + epsilon)

    next_resid_a = raw_a / beta
    next_resid_b = raw_b / beta
    next_basis = raw_v / alpha_next
    rho_total = jnp.sqrt(rhobar * rhobar + beta * beta)
    cosine = rhobar / rho_total
    sine = beta / rho_total
    theta = sine * alpha_next
    phi_value = cosine * phibar
    next_solution = solution + phi_value / rho_total * search
    next_search = next_basis - theta / rho_total * search
    return (next_solution, next_search, next_basis, next_resid_a, next_resid_b)


def solution(mesh):
    placed = (
        P(None, "row", "col"),
        P(None, "row", "col"),
        P(None, "row", "col"),
        P("row", "col"),
        P("row", "col"),
        P(),
        P(),
        P(),
        P("row", "col"),
        P("row", "col"),
        P("row", "col"),
    )
    return jax.shard_map(
        body,
        mesh=mesh,
        in_specs=placed,
        out_specs=(
            P(None, "row", "col"),
            P(None, "row", "col"),
            P(None, "row", "col"),
            P("row", "col"),
            P("row", "col"),
        ),
        check_vma=False,
    )
```
